32 devices in a mesh: dp: 16 (over z, x, core), inner: 2 (over y).
Axes of the slice: x: 2, y: 2, z: 4, core: 2. Of those that a mesh axis runs over, the one named last changes fastest.
Arguments:
- grad_parts: bfloat16 [32, 20, 256, 256], P(('dp', 'inner')), may hold values from -0.125 to 0.125
- owner: int32 [20], replicated, may hold values from 0 to 15, as said below
- weights: bfloat16 [32, 256, 256], P('dp'), may hold values from -0.375 to 0.375
- first_moment: float32 [32, 256, 256], P('dp'), may hold values from -1.5 to 1.5
- second_moment: float32 [32, 256, 256], P('dp'), may hold values from 0.01 to 0.1
- left_stats: float32 [32, 256, 256], P('dp'), may hold values from -5 to 10, as said below
- right_stats: float32 [32, 256, 256], P('dp'), may hold values from -5 to 10, as said below
- left_basis: float32 [32, 256, 256], P('dp'), may hold values from -0.375 to 0.375
- right_basis: float32 [32, 256, 256], P('dp'), may hold values from -0.375 to 0.375
Outputs:
- new_weights: bfloat16 [20, 256, 256], replicated
- first_out: float32 [32, 256, 256], P('dp')
- second_out: float32 [32, 256, 256], P('dp')
- left_stats_out: float32 [32, 256, 256], P('dp')
- right_stats_out: float32 [32, 256, 256], P('dp')
- left_basis_out: float32 [32, 256, 256], P('dp')
- right_basis_out: float32 [32, 256, 256], P('dp')
The draws below stay inside these ranges and needn't reach their ends.
Inputs may be any that keep to these rules, and one draw needn't show every extreme that they name: owner[b] is the dp index holding block b's state; no dp index owns more than 2 blocks, and one owns exactly 2. left_stats is symmetric. right_stats is symmetric.
All inputs are finite; a program needn't handle non-finite values.
Results may differ from the reference program's by a relative error of at most 0.002.
Values may be sent and summed in bfloat16 or wider, within the bound.
A program may use at most 64 MiB of HBM per device.

```python
import math
import jax
import jax.numpy as jnp
from jax import lax

KV = 256
NS_STEPS = 5
NB = 20
CAP = 2
SLOTS = 32
REPLICAS = 32


def draw_owner(key, part):
    first_key, second_key = jax.random.split(key)
    visiting = jax.random.permutation(first_key, SLOTS).astype(jnp.int32)
    position = jnp.argsort(visiting, stable=True).astype(jnp.int32)
    favoured = visiting[0] // CAP
    slot_index = jnp.arange(SLOTS, dtype=jnp.int32)
    ranked = position - SLOTS * (slot_index // CAP == favoured).astype(jnp.int32)
    chosen = jnp.argsort(ranked, stable=True).astype(jnp.int32)[:NB]
    shuffle = jax.random.permutation(second_key, NB).astype(jnp.int32)
    return (chosen[shuffle] // CAP).astype(jnp.int32)


def symmetric_draw(key):
    scale_key, noise_key = jax.random.split(key)
    scales = jnp.exp(jax.random.uniform(scale_key, (SLOTS, KV), jnp.float32, jnp.log(0.3), jnp.log(3.0)))
    noise = jnp.clip(jax.random.normal(noise_key, (SLOTS, KV, KV), jnp.float32), -4.0, 4.0)
    noise = 0.5 * (noise + jnp.swapaxes(noise, 1, 2))
    roots = jnp.sqrt(scales)
    offdiag = 0.125 * noise * roots[:, :, None] * roots[:, None, :]
    identity = jnp.eye(KV, dtype=jnp.float32)
    return offdiag * (1.0 - identity) + identity * scales[:, :, None]


def draw_left_stats(key, part):
    return symmetric_draw(jax.random.fold_in(key, 11))


def draw_right_stats(key, part):
    return symmetric_draw(jax.random.fold_in(key, 23))


def spiked(result, rng, source, target, blocks, factor):
    def block_of(axis_at):
        return (jnp.arange(result.shape[axis_at]) // (result.shape[axis_at] // blocks)).reshape((-1,) + (1,) * (result.ndim - 1 - axis_at))

    first = jax.random.permutation(rng, blocks)[block_of(target)]
    second = (block_of(target) + blocks // 2) % blocks
    return jnp.where((block_of(source) == first) | (block_of(source) == second), factor * result, result)


def steps_of(own_key, extent, shards, smallest, largest):
    def one(dim, parts):
        draws = jax.random.uniform(jax.random.fold_in(jax.random.fold_in(own_key, 6), dim), (parts,), jnp.float32, smallest / len(shards), largest / len(shards))
        return jnp.repeat(jnp.exp(draws), extent[dim] // parts).reshape((-1,) + (1,) * (len(extent) - dim - 1))

    loudness = one(*shards[0])
    for cut in shards[1:]:
        loudness = loudness * one(*cut)
    return loudness


def normal_values(own_key, shape, scale, limit, pieces=(), held_as=jnp.bfloat16):
    values = jax.random.normal(own_key, shape, jnp.float32) * scale
    if len(pieces) > 0:
        values = steps_of(own_key, shape, pieces, -0.22, 0.18) * values
    return jnp.clip(values, min=-limit, max=limit).astype(held_as)


def bell_draw_with(rng, shape, width, bound, shards, heavy, kind=jnp.bfloat16):
    values = width * jax.random.normal(rng, shape, jnp.float32)
    if shards:
        values = values * steps_of(rng, shape, shards, -0.22, 0.18)
    return jnp.clip(spiked(values, jax.random.fold_in(rng, 3), *heavy), -bound, bound).astype(kind)


def setup_inputs(seed: int = 0) -> dict:
    arg_keys = jax.random.split(jax.random.key(seed), 10)
    grad_parts = bell_draw_with(arg_keys[0], (REPLICAS, NB, KV, KV), 0.015625, 0.125, ((0, 32),), (0, 1, 4, 2.0))
    owner = draw_owner(jax.random.fold_in(arg_keys[9], 71), 0)
    weights = normal_values(arg_keys[2], (SLOTS, KV, KV), KV ** -0.5, 0.375, ((0, 16),))
    first_moment = normal_values(arg_keys[3], (SLOTS, KV, KV), 0.25, 1.5, ((0, 16),), jnp.float32)
    second_moment = jnp.clip(jnp.exp(math.log(0.1) - 2.3025851 * jax.random.uniform(arg_keys[4], (SLOTS, KV, KV), jnp.float32) ** steps_of(arg_keys[4], (SLOTS, KV, KV), ((0, 16),), -0.2, 0.2)), 0.01, 0.1)
    left_stats = draw_left_stats(jax.random.fold_in(arg_keys[9], 71), 0)
    right_stats = draw_right_stats(jax.random.fold_in(arg_keys[9], 71), 0)
    left_basis = normal_values(arg_keys[7], (SLOTS, KV, KV), KV ** -0.5, 0.375, ((0, 16),), jnp.float32)
    right_basis = normal_values(arg_keys[8], (SLOTS, KV, KV), KV ** -0.5, 0.375, ((0, 16),), jnp.float32)
    return dict(grad_parts=grad_parts, owner=owner, weights=weights, first_moment=first_moment, second_moment=second_moment, left_stats=left_stats, right_stats=right_stats, left_basis=left_basis, right_basis=right_basis)


SMOOTHING = 0.95
BIAS_CORRECTION = 1.0 - 0.95 ** 10
LEARNING_RATE = 0.01
PRECISE = lax.Precision.HIGHEST

def slot_targets(owner):
    count = owner.shape[0]
    index = jnp.arange(count, dtype=jnp.int32)
    earlier = (owner[:, None] == owner[None, :]) & (index[None, :] < index[:, None])
    return (owner * CAP + lax.optimization_barrier(jnp.sum(earlier.astype(jnp.int32), axis=1))).astype(jnp.int32)

def orthonormalize(power):
    norm = jnp.sqrt(lax.optimization_barrier(jnp.sum(power * power, axis=(1, 2), keepdims=True)))
    current = power / (norm + 1e-06)
    for step in range(NS_STEPS):
        square = jnp.einsum('cij,ckj->cik', current, current, precision=PRECISE)
        current = 1.5 * current - 0.5 * jnp.einsum('cik,ckj->cij', square, current, precision=PRECISE)
    return current

def reference(grad_parts, owner, weights, first_moment, second_moment, left_stats, right_stats, left_basis, right_basis):

    def accumulate(total, piece):
        return (total + piece.astype(jnp.float32), None)
    summed, unused = lax.scan(accumulate, jnp.zeros(grad_parts.shape[1:], jnp.float32), grad_parts)
    target = slot_targets(owner)
    grad = jnp.zeros(first_moment.shape, jnp.float32).at[target].set(summed)
    half_turn = jnp.einsum('cik,cil->ckl', left_basis, grad, precision=PRECISE)
    rotated = jnp.einsum('ckl,clm->ckm', half_turn, right_basis, precision=PRECISE)
    first_out = SMOOTHING * first_moment + (1.0 - SMOOTHING) * rotated
    second_out = SMOOTHING * second_moment + (1.0 - SMOOTHING) * rotated * rotated
    direction = first_out / BIAS_CORRECTION / (jnp.sqrt(second_out / BIAS_CORRECTION) + 1e-08)
    back_turn = jnp.einsum('cik,ckl->cil', left_basis, direction, precision=PRECISE)
    update = jnp.einsum('cil,cml->cim', back_turn, right_basis, precision=PRECISE)
    new_slots = (weights.astype(jnp.float32) - LEARNING_RATE * update).astype(jnp.bfloat16)
    new_weights = new_slots[target]
    left_stats_out = SMOOTHING * left_stats + (1.0 - SMOOTHING) * jnp.einsum('cil,cjl->cij', grad, grad, precision=PRECISE)
    right_stats_out = SMOOTHING * right_stats + (1.0 - SMOOTHING) * jnp.einsum('cli,clj->cij', grad, grad, precision=PRECISE)
    left_power = jnp.einsum('cij,cjk->cik', left_stats_out, left_basis, precision=PRECISE)
    right_power = jnp.einsum('cij,cjk->cik', right_stats_out, right_basis, precision=PRECISE)
    left_basis_out = orthonormalize(left_power)
    right_basis_out = orthonormalize(right_power)
    return (new_weights, first_out, second_out, left_stats_out, right_stats_out, left_basis_out, right_basis_out)
```

```python
import functools

import jax
import jax.numpy as jnp
from jax import lax
from jax.experimental import pallas as pl
from jax.experimental.pallas import tpu as pltpu
from jax.sharding import PartitionSpec as P

NS_STEPS = 5


SMOOTHING = 0.95
BIAS_CORRECTION = 1.0 - 0.95**10
LEARNING_RATE = 0.01
PRECISE = lax.Precision.HIGH
MESH = pl.DeviceIdType.MESH
CORES = 2
XS = 2
PIECES = 4


def slot_numbers(owner):
    count = owner.shape[0]
    index = jnp.arange(count, dtype=jnp.int32)
    earlier = (owner[:, None] == owner[None, :]) & (index[None, :] < index[:, None])
    return jnp.sum(earlier.astype(jnp.int32), axis=1)


def position(inner_count):
    d = lax.axis_index("dp")
    c = lax.rem(d, CORES)
    x = lax.rem(d // CORES, XS)
    z = d // (CORES * XS)
    i = lax.axis_index("inner")
    return z, x, c, i


def dp_of(z, x, c):
    return (z * XS + x) * CORES + c


class Copies:
    def __init__(self, send, recv):
        self.send, self.recv, self.made = send, recv, []

    def start(self, src, dst, device):
        n = len(self.made)
        copy = pltpu.make_async_remote_copy(
            src_ref=src,
            dst_ref=dst,
            send_sem=self.send.at[n],
            recv_sem=self.recv.at[n],
            device_id=device,
            device_id_type=MESH,
        )
        copy.start()
        self.made.append(copy)
        return copy

    def finish(self):
        for copy in self.made:
            copy.wait_send()


def greet(devices):
    barrier = pltpu.get_barrier_semaphore()
    for device in devices:
        pl.semaphore_signal(barrier, inc=1, device_id=device, device_id_type=MESH)
    pl.semaphore_wait(barrier, len(devices))


def plane_offsets(inner_count):
    return [
        (dx, dc, di)
        for di in range(inner_count)
        for dx in range(XS)
        for dc in range(CORES)
        if (dx, dc, di) != (0, 0, 0)
    ]


def reduce_kernel(
    zs, inner, cap, nb, rows,
    block_ref, valid_ref, g_ref, out_ref,
    b1, s1, r2a, s2a, f2a, r3a, r2b, s2b, f2b, r3b, total, zsend, zown, zrecv, psend, gbuf,
    send, recv,
):
    z, x, c, i = position(inner)
    f32, bf16 = jnp.float32, jnp.bfloat16
    here = dp_of(z, x, c)
    core_peer = (dp_of(z, x, 1 - c), i)
    x_peer = (dp_of(z, 1 - x, c), i)

    def inner_peer(m):
        return (here, lax.rem(i + m, inner))

    def z_peer(k):
        return (dp_of(lax.rem(z + k, zs), x, c), i)

    def plane_peer(dx, dc, di):
        return (dp_of(z, lax.rem(x + dx, XS), lax.rem(c + dc, CORES)), lax.rem(i + di, inner))

    offsets = plane_offsets(inner)
    greet([plane_peer(*o) for o in offsets] + [z_peer(k) for k in range(1, zs)])

    copies = Copies(send, recv)
    half = nb // 2
    size = nb // PIECES
    pieces = []
    for p in range(PIECES // 2):
        pieces += [(True, p * size), (False, half + p * size)]

    first = [
        copies.start(g_ref.at[pl.ds(lo, size), 1 - c], b1.at[pl.ds(lo, size)], core_peer)
        for _, lo in pieces
    ]
    second = []
    for (inner_first, lo), arrived in zip(pieces, first):
        arrived.wait_recv()

        @pl.loop(lo, lo + size)
        def _(b):
            s1[b] = (g_ref[b, c].astype(f32) + b1[b].astype(f32)).astype(bf16)

        if inner_first:
            second.append([
                copies.start(
                    s1.at[pl.ds(lo, size), :, lax.rem(i + m, inner)],
                    r2a.at[m - 1, pl.ds(lo, size)],
                    inner_peer(m),
                )
                for m in range(1, inner)
            ])
        else:
            second.append([
                copies.start(
                    s1.at[pl.ds(lo, size), 1 - x], r2b.at[pl.ds(lo - half, size)], x_peer
                )
            ])
    third = []
    for (inner_first, lo), arrived in zip(pieces, second):
        for copy in arrived:
            copy.wait_recv()
        if inner_first:

            @pl.loop(lo, lo + size)
            def _(b):
                value = g_ref[b, c, :, i].astype(f32) + b1[b, :, i].astype(f32)
                for m in range(1, inner):
                    value = value + r2a[m - 1, b].astype(f32)
                f2a[b] = value
                s2a[b] = value.astype(bf16)

            third.append([
                copies.start(s2a.at[pl.ds(lo, size), 1 - x], r3a.at[pl.ds(lo, size)], x_peer)
            ])
        else:

            @pl.loop(lo, lo + size)
            def _(b):
                value = g_ref[b, c, x].astype(f32) + b1[b, x].astype(f32)
                value = value + r2b[b - half].astype(f32)
                f2b[b - half] = value
                s2b[b - half] = value.astype(bf16)

            third.append([
                copies.start(
                    s2b.at[pl.ds(lo - half, size), lax.rem(i + m, inner)],
                    r3b.at[m - 1, pl.ds(lo - half, size)],
                    inner_peer(m),
                )
                for m in range(1, inner)
            ])
    for (inner_first, lo), arrived in zip(pieces, third):
        for copy in arrived:
            copy.wait_recv()
        if inner_first:

            @pl.loop(lo, lo + size)
            def _(b):
                total[b] = f2a[b, x] + r3a[b].astype(f32)

        else:

            @pl.loop(lo, lo + size)
            def _(b):
                value = f2b[b - half, i]
                for m in range(1, inner):
                    value = value + r3b[m - 1, b - half].astype(f32)
                total[b] = value

    plane = XS * CORES * cap

    def slot_value(slot):
        value = total[block_ref[slot]]
        return jnp.where(valid_ref[slot] > 0, value, jnp.zeros_like(value))

    fourth = []
    for k in range(1, zs):
        there = lax.rem(z + k, zs)

        @pl.loop(0, plane)
        def _(s):
            zsend[k - 1, s] = slot_value(there * plane + s).astype(bf16)

        fourth.append(copies.start(zsend.at[k - 1], zrecv.at[k - 1], z_peer(k)))

    @pl.loop(0, plane)
    def _(s):
        zown[s] = slot_value(z * plane + s)

    for copy in fourth:
        copy.wait_recv()

    @pl.loop(0, plane)
    def _(s):
        value = zown[s]
        for k in range(1, zs):
            value = value + zrecv[k - 1, s].astype(f32)
        psend[s] = value.astype(bf16)

    share = (c * XS + x) * inner + i
    fifth = []
    for dx, dc, di in offsets:
        to = lax.rem(x + dx, XS) * CORES + lax.rem(c + dc, CORES)
        fifth.append(
            copies.start(
                psend.at[pl.ds(to * cap, cap)], gbuf.at[share], plane_peer(dx, dc, di)
            )
        )
    gbuf[share] = psend[pl.ds((x * CORES + c) * cap, cap)]
    for copy in fifth:
        copy.wait_recv()
    for s in range(CORES * XS * inner):
        out_ref[:, s * rows : (s + 1) * rows, :] = gbuf[s].astype(f32)
    copies.finish()


def reduce_grads(zs, inner, cap, grad_parts, block, valid):
    nb, order = grad_parts.shape[0], grad_parts.shape[1]
    rows = order // (CORES * XS * inner)
    half = nb // 2
    plane = XS * CORES * cap
    f32, bf16 = jnp.float32, jnp.bfloat16
    tile = (rows, order)
    g = grad_parts.reshape(nb, CORES, XS, inner, rows, order)
    offsets = len(plane_offsets(inner))
    count = PIECES + PIECES * inner + (zs - 1) + offsets
    smem = pl.BlockSpec(memory_space=pltpu.SMEM)
    vmem = pl.BlockSpec(memory_space=pltpu.VMEM)
    return pl.pallas_call(
        functools.partial(reduce_kernel, zs, inner, cap, nb, rows),
        out_shape=jax.ShapeDtypeStruct((cap, order, order), f32),
        in_specs=[smem, smem, vmem],
        out_specs=vmem,
        scratch_shapes=[
            pltpu.VMEM((nb, XS, inner) + tile, bf16),
            pltpu.VMEM((nb, XS, inner) + tile, bf16),
            pltpu.VMEM((inner - 1, half, XS) + tile, bf16),
            pltpu.VMEM((half, XS) + tile, bf16),
            pltpu.VMEM((half, XS) + tile, f32),
            pltpu.VMEM((half,) + tile, bf16),
            pltpu.VMEM((half, inner) + tile, bf16),
            pltpu.VMEM((half, inner) + tile, bf16),
            pltpu.VMEM((half, inner) + tile, f32),
            pltpu.VMEM((inner - 1, half) + tile, bf16),
            pltpu.VMEM((nb,) + tile, f32),
            pltpu.VMEM((zs - 1, plane) + tile, bf16),
            pltpu.VMEM((plane,) + tile, f32),
            pltpu.VMEM((zs - 1, plane) + tile, bf16),
            pltpu.VMEM((plane,) + tile, bf16),
            pltpu.VMEM((CORES * XS * inner, cap) + tile, bf16),
            pltpu.SemaphoreType.DMA((count,)),
            pltpu.SemaphoreType.DMA((count,)),
        ],
        compiler_params=pltpu.CompilerParams(collective_id=0, has_side_effects=True),
    )(block, valid, g)


def gather_kernel(zs, inner, cap, nb, rows, place_ref, mine_ref, out_ref, held, send, recv):
    z, x, c, i = position(inner)
    here = dp_of(z, x, c)
    core_peer = (dp_of(z, x, 1 - c), i)
    x_peer = (dp_of(z, 1 - x, c), i)

    def inner_peer(m):
        return (here, lax.rem(i + m, inner))

    def z_peer(k):
        return (dp_of(lax.rem(z + k, zs), x, c), i)

    greet(
        [core_peer, x_peer]
        + [inner_peer(m) for m in range(1, inner)]
        + [z_peer(k) for k in range(1, zs)]
    )
    copies = Copies(send, recv)
    own = held.at[z, x, i, c]
    along_z = [copies.start(mine_ref, own, z_peer(k)) for k in range(1, zs)]
    to_x, to_inner, to_core = [], [], []
    for k in range(zs):
        from_z = lax.rem(z + zs - k, zs)
        slot = held.at[from_z, x, i, c]
        if k > 0:
            along_z[k - 1].wait_recv()
        src = mine_ref if k == 0 else slot
        to_x.append(copies.start(src, slot, x_peer))
        to_inner.append([copies.start(src, slot, inner_peer(m)) for m in range(1, inner)])
        to_core.append(copies.start(src, slot, core_peer))
    held[z, x, i, c] = mine_ref[...]
    corner = []
    for k in range(zs):
        from_z = lax.rem(z + zs - k, zs)
        slot = held.at[from_z, 1 - x, i, c]
        to_x[k].wait_recv()
        ahead = [
            copies.start(slot.at[0], slot.at[0], inner_peer(m)) for m in range(1, inner)
        ]
        to_core.append(copies.start(slot, slot, core_peer))
        for m in range(1, inner):
            from_i = lax.rem(i + inner - m, inner)
            slot = held.at[from_z, x, from_i, c]
            to_inner[k][m - 1].wait_recv()
            across = copies.start(slot.at[1], slot.at[1], x_peer)
            to_core.append(copies.start(slot, slot, core_peer))
            corner.append((from_z, from_i, ahead[m - 1], across))
    for from_z, from_i, ahead, across in corner:
        slot = held.at[from_z, 1 - x, from_i, c]
        ahead.wait_recv()
        to_core.append(copies.start(slot.at[0], slot.at[0], core_peer))
        across.wait_recv()
        to_core.append(copies.start(slot.at[1], slot.at[1], core_peer))
    for copy in to_core:
        copy.wait_recv()

    @pl.loop(0, nb)
    def _(b):
        bz, bx, bc, bk = (place_ref[n, b] for n in range(4))
        for part in range(inner):
            for h in range(2):
                lo = (part * 2 + h) * rows
                out_ref[b, lo : lo + rows, :] = held[bz, bx, part, bc, h, bk]

    copies.finish()


def gather_weights(zs, inner, nb, new_rows, owner, slot_number):
    cap, order = new_rows.shape[0], new_rows.shape[1]
    rows = order // (inner * 2)
    mine = lax.dynamic_slice_in_dim(
        new_rows, lax.axis_index("inner") * 2 * rows, 2 * rows, 1
    )
    mine = mine.reshape(cap, 2, rows, order).swapaxes(0, 1)
    place = jnp.stack(
        [owner // (XS * CORES), (owner // CORES) % XS, owner % CORES, slot_number]
    ).astype(jnp.int32)
    others = inner - 1
    count = (zs - 1) + zs * (2 + others) + zs * (1 + 3 * others) + zs * 2 * others
    smem = pl.BlockSpec(memory_space=pltpu.SMEM)
    vmem = pl.BlockSpec(memory_space=pltpu.VMEM)
    return pl.pallas_call(
        functools.partial(gather_kernel, zs, inner, cap, nb, rows),
        out_shape=jax.ShapeDtypeStruct((nb, order, order), jnp.bfloat16),
        in_specs=[smem, vmem],
        out_specs=vmem,
        scratch_shapes=[
            pltpu.VMEM((zs, XS, inner, CORES, 2, cap, rows, order), jnp.bfloat16),
            pltpu.SemaphoreType.DMA((count,)),
            pltpu.SemaphoreType.DMA((count,)),
        ],
        compiler_params=pltpu.CompilerParams(collective_id=1, has_side_effects=True),
    )(place, mine)


def orthonormalize(power):
    norm = jnp.sqrt(jnp.sum(power * power, axis=(1, 2), keepdims=True))
    current = power / (norm + 1e-06)
    for step in range(NS_STEPS):
        square = jnp.einsum("cij,ckj->cik", current, current, precision=PRECISE)
        current = 1.5 * current - 0.5 * jnp.einsum(
            "cik,ckj->cij", square, current, precision=PRECISE
        )
    return current


def local(
    grad_parts,
    owner,
    weights,
    first_moment,
    second_moment,
    left_stats,
    right_stats,
    left_basis,
    right_basis,
):
    dp_count = lax.axis_size("dp")
    inner_count = lax.axis_size("inner")
    capacity = weights.shape[0]
    block_count = owner.shape[0]
    zs = dp_count // (XS * CORES)
    slot_number = slot_numbers(owner)
    target = owner * capacity + slot_number
    match = jnp.arange(dp_count * capacity, dtype=jnp.int32)[:, None] == target[None, :]
    valid = jnp.sum(match.astype(jnp.int32), axis=1)
    block = jnp.sum(
        jnp.where(match, jnp.arange(block_count, dtype=jnp.int32)[None, :], 0), axis=1
    )
    grad = reduce_grads(zs, inner_count, capacity, grad_parts[0], block, valid)
    half_turn = jnp.einsum("cik,cil->ckl", left_basis, grad, precision=PRECISE)
    rotated = jnp.einsum("ckl,clm->ckm", half_turn, right_basis, precision=PRECISE)
    first_out = SMOOTHING * first_moment + (1.0 - SMOOTHING) * rotated
    second_out = SMOOTHING * second_moment + (1.0 - SMOOTHING) * rotated * rotated
    direction = first_out / BIAS_CORRECTION / (jnp.sqrt(second_out / BIAS_CORRECTION) + 1e-08)
    back_turn = jnp.einsum("cik,ckl->cil", left_basis, direction, precision=PRECISE)
    update = jnp.einsum("cil,cml->cim", back_turn, right_basis, precision=PRECISE)
    new_rows = (weights.astype(jnp.float32) - LEARNING_RATE * update).astype(jnp.bfloat16)
    new_weights = gather_weights(zs, inner_count, block_count, new_rows, owner, slot_number)
    left_stats_out = SMOOTHING * left_stats + (1.0 - SMOOTHING) * jnp.einsum(
        "cil,cjl->cij", grad, grad, precision=PRECISE
    )
    right_stats_out = SMOOTHING * right_stats + (1.0 - SMOOTHING) * jnp.einsum(
        "cli,clj->cij", grad, grad, precision=PRECISE
    )
    left_power = jnp.einsum("cij,cjk->cik", left_stats_out, left_basis, precision=PRECISE)
    right_power = jnp.einsum("cij,cjk->cik", right_stats_out, right_basis, precision=PRECISE)
    left_basis_out = orthonormalize(left_power)
    right_basis_out = orthonormalize(right_power)
    return (
        new_weights,
        first_out,
        second_out,
        left_stats_out,
        right_stats_out,
        left_basis_out,
        right_basis_out,
    )


def solution(mesh):
    dp = P("dp", None, None)
    in_specs = (P(("dp", "inner"), None, None, None), P()) + (dp,) * 7
    out_specs = (P(),) + (dp,) * 6
    return jax.shard_map(local, mesh=mesh, in_specs=in_specs, out_specs=out_specs, check_vma=False)
```

```python
import functools

import jax
import jax.numpy as jnp
from jax import lax
from jax.experimental import pallas as pl
from jax.experimental.pallas import tpu as pltpu
from jax.sharding import PartitionSpec as P

NS_STEPS = 5


SMOOTHING = 0.95
BIAS_CORRECTION = 1.0 - 0.95**10
LEARNING_RATE = 0.01
MESH = pl.DeviceIdType.MESH
CORES = 2
XS = 2
PIECES = 4


def position(inner_count):
    d = lax.axis_index("dp")
    c = lax.rem(d, CORES)
    x = lax.rem(d // CORES, XS)
    z = d // (CORES * XS)
    i = lax.axis_index("inner")
    return z, x, c, i


def dp_of(z, x, c):
    return (z * XS + x) * CORES + c


class Copies:
    def __init__(self, send, recv):
        self.send, self.recv, self.made = send, recv, []

    def start(self, src, dst, device):
        n = len(self.made)
        copy = pltpu.make_async_remote_copy(
            src_ref=src,
            dst_ref=dst,
            send_sem=self.send.at[n],
            recv_sem=self.recv.at[n],
            device_id=device,
            device_id_type=MESH,
        )
        copy.start()
        self.made.append(copy)
        return copy

    def finish(self):
        for copy in self.made:
            copy.wait_send()


def greet(devices):
    barrier = pltpu.get_barrier_semaphore()
    for device in devices:
        pl.semaphore_signal(barrier, inc=1, device_id=device, device_id_type=MESH)
    pl.semaphore_wait(barrier, len(devices))


def plane_offsets(inner_count):
    return [
        (dx, dc, di)
        for di in range(inner_count)
        for dx in range(XS)
        for dc in range(CORES)
        if (dx, dc, di) != (0, 0, 0)
    ]


def parts_of(value):
    high = value.astype(jnp.bfloat16)
    return high, (value - high.astype(jnp.float32)).astype(jnp.bfloat16)


def product(left, right, dims):
    def dot(a, b):
        return lax.dot_general(a, b, (dims, ((), ())), preferred_element_type=jnp.float32)

    total = dot(left[0], right[0])
    if len(right) > 1:
        total = total + dot(left[0], right[1])
    if len(left) > 1:
        total = total + dot(left[1], right[0])
    return total


PLAIN = ((1,), (0,))
LEFT_T = ((0,), (0,))
RIGHT_T = ((1,), (1,))


def step_kernel(
    zs, inner, cap, nb, rows, wide,
    owner_ref, g_ref, w_hbm, m1_hbm, m2_hbm, ls_hbm, rs_hbm, lb_hbm, rb_hbm,
    out_ref, m1_ref, m2_ref, ls_ref, rs_ref, lb_ref, rb_ref,
    block_ref, number_ref,
    w_in, m1_in, m2_in, ls_in, rs_in, lb_in, rb_in,
    b1, s1, r2a, s2a, f2a, r3a, r2b, s2b, f2b, r3b, total, zsend, zown, zrecv, psend, gbuf,
    grads, fresh, held,
    load, send, recv,
):
    z, x, c, i = position(inner)
    f32, bf16 = jnp.float32, jnp.bfloat16
    here = dp_of(z, x, c)
    core_peer = (dp_of(z, x, 1 - c), i)
    x_peer = (dp_of(z, 1 - x, c), i)

    def inner_peer(m):
        return (here, lax.rem(i + m, inner))

    def z_peer(k):
        return (dp_of(lax.rem(z + k, zs), x, c), i)

    def plane_peer(dx, dc, di):
        return (dp_of(z, lax.rem(x + dx, XS), lax.rem(c + dc, CORES)), lax.rem(i + di, inner))

    offsets = plane_offsets(inner)
    loads = []
    for n, (src, dst) in enumerate([
        (w_hbm, w_in), (m1_hbm, m1_in), (m2_hbm, m2_in), (ls_hbm, ls_in),
        (rs_hbm, rs_in), (lb_hbm, lb_in), (rb_hbm, rb_in),
    ]):
        loads.append(pltpu.make_async_copy(src, dst, load.at[n]))
    greet([plane_peer(*o) for o in offsets] + [z_peer(k) for k in range(1, zs)])

    copies = Copies(send, recv)
    half = nb // 2
    size = nb // PIECES
    pieces = []
    for p in range(PIECES // 2):
        pieces += [(True, p * size), (False, half + p * size)]

    first = [
        copies.start(g_ref.at[pl.ds(lo, size), 1 - c], b1.at[pl.ds(lo, size)], core_peer)
        for _, lo in pieces
    ]
    for copy in loads:
        copy.start()

    @pl.loop(0, zs * XS * CORES)
    def _(d):
        def look(b, state):
            seen, found = state
            hit = owner_ref[b] == d
            found = tuple(
                jnp.where(hit & (seen == n), b, old) for n, old in enumerate(found)
            )
            return seen + jnp.where(hit, 1, 0), found

        none = tuple(jnp.int32(-1) for _ in range(cap))
        _, found = lax.fori_loop(0, nb, look, (jnp.int32(0), none))
        for n in range(cap):
            block_ref[d * cap + n] = found[n]

    @pl.loop(0, nb)
    def _(b):
        def look(other, seen):
            return seen + jnp.where((owner_ref[other] == owner_ref[b]) & (other < b), 1, 0)

        number_ref[b] = lax.fori_loop(0, nb, look, jnp.int32(0))

    second = []
    for (inner_first, lo), arrived in zip(pieces, first):
        arrived.wait_recv()

        @pl.loop(lo, lo + size)
        def _(b):
            s1[b] = (g_ref[b, c].astype(f32) + b1[b].astype(f32)).astype(bf16)

        if inner_first:
            second.append([
                copies.start(
                    s1.at[pl.ds(lo, size), :, lax.rem(i + m, inner)],
                    r2a.at[m - 1, pl.ds(lo, size)],
                    inner_peer(m),
                )
                for m in range(1, inner)
            ])
        else:
            second.append([
                copies.start(
                    s1.at[pl.ds(lo, size), 1 - x], r2b.at[pl.ds(lo - half, size)], x_peer
                )
            ])
    third = []
    for (inner_first, lo), arrived in zip(pieces, second):
        for copy in arrived:
            copy.wait_recv()
        if inner_first:

            @pl.loop(lo, lo + size)
            def _(b):
                value = g_ref[b, c, :, i].astype(f32) + b1[b, :, i].astype(f32)
                for m in range(1, inner):
                    value = value + r2a[m - 1, b].astype(f32)
                f2a[b] = value
                s2a[b] = value.astype(bf16)

            third.append([
                copies.start(s2a.at[pl.ds(lo, size), 1 - x], r3a.at[pl.ds(lo, size)], x_peer)
            ])
        else:

            @pl.loop(lo, lo + size)
            def _(b):
                value = g_ref[b, c, x].astype(f32) + b1[b, x].astype(f32)
                value = value + r2b[b - half].astype(f32)
                f2b[b - half] = value
                s2b[b - half] = value.astype(bf16)

            third.append([
                copies.start(
                    s2b.at[pl.ds(lo - half, size), lax.rem(i + m, inner)],
                    r3b.at[m - 1, pl.ds(lo - half, size)],
                    inner_peer(m),
                )
                for m in range(1, inner)
            ])
    for (inner_first, lo), arrived in zip(pieces, third):
        for copy in arrived:
            copy.wait_recv()
        if inner_first:

            @pl.loop(lo, lo + size)
            def _(b):
                total[b] = f2a[b, x] + r3a[b].astype(f32)

        else:

            @pl.loop(lo, lo + size)
            def _(b):
                value = f2b[b - half, i]
                for m in range(1, inner):
                    value = value + r3b[m - 1, b - half].astype(f32)
                total[b] = value

    plane = XS * CORES * cap

    def slot_value(slot):
        block = block_ref[slot]
        value = total[jnp.maximum(block, 0)]
        return jnp.where(block >= 0, value, jnp.zeros_like(value))

    fourth = []
    for k in range(1, zs):
        there = lax.rem(z + k, zs)

        @pl.loop(0, plane)
        def _(s):
            zsend[k - 1, s] = slot_value(there * plane + s).astype(bf16)

        fourth.append(copies.start(zsend.at[k - 1], zrecv.at[k - 1], z_peer(k)))

    @pl.loop(0, plane)
    def _(s):
        zown[s] = slot_value(z * plane + s)

    for copy in fourth:
        copy.wait_recv()

    @pl.loop(0, plane)
    def _(s):
        value = zown[s]
        for k in range(1, zs):
            value = value + zrecv[k - 1, s].astype(f32)
        psend[s] = value.astype(bf16)

    share = (c * XS + x) * inner + i
    fifth = []
    for dx, dc, di in offsets:
        to = lax.rem(x + dx, XS) * CORES + lax.rem(c + dc, CORES)
        fifth.append(
            copies.start(
                psend.at[pl.ds(to * cap, cap)], gbuf.at[share], plane_peer(dx, dc, di)
            )
        )
    gbuf[share] = psend[pl.ds((x * CORES + c) * cap, cap)]
    for copy in fifth:
        copy.wait_recv()
    for s in range(CORES * XS * inner):
        grads[:, s * rows : (s + 1) * rows, :] = gbuf[s].astype(f32)
    for copy in loads:
        copy.wait()

    for k in range(cap):
        lb, rb = parts_of(lb_in[k]), parts_of(rb_in[k])
        half_turn = product(lb, (grads[k].astype(bf16),), LEFT_T)
        rotated = product(parts_of(half_turn), rb, PLAIN)
        first = SMOOTHING * m1_in[k] + (1.0 - SMOOTHING) * rotated
        second = SMOOTHING * m2_in[k] + (1.0 - SMOOTHING) * rotated * rotated
        m1_ref[k] = first
        m2_ref[k] = second
        direction = first / BIAS_CORRECTION / (jnp.sqrt(second / BIAS_CORRECTION) + 1e-08)
        back_turn = product(lb, parts_of(direction), PLAIN)
        update = product(parts_of(back_turn), rb, RIGHT_T)
        new = (w_in[k].astype(f32) - LEARNING_RATE * update).astype(bf16)
        for part in range(inner):
            for h in range(2):
                lo = (part * 2 + h) * wide
                fresh[part, h, k] = new[lo : lo + wide]

    def powers():
        @pl.loop(0, cap)
        def _(k):
            g = (grads[k].astype(bf16),)
            for in_ref, stats_ref, basis_in, basis_ref, dims in (
                (ls_in, ls_ref, lb_in, lb_ref, RIGHT_T),
                (rs_in, rs_ref, rb_in, rb_ref, LEFT_T),
            ):
                stats = SMOOTHING * in_ref[k] + (1.0 - SMOOTHING) * product(g, g, dims)
                stats_ref[k] = stats
                power = product(parts_of(stats), parts_of(basis_in[k]), PLAIN)
                norm = jnp.sqrt(jnp.sum(power * power, axis=(0, 1), keepdims=True))
                basis_ref[k] = power / (norm + 1e-06)

    def newton_schulz():
        @pl.loop(0, cap)
        def _(k):
            for basis_ref in (lb_ref, rb_ref):
                current = basis_ref[k]
                parts = parts_of(current)
                square = product(parts, parts, RIGHT_T)
                cubic = product(parts_of(square), parts, PLAIN)
                basis_ref[k] = 1.5 * current - 0.5 * cubic

    work = [powers] + [newton_schulz] * NS_STEPS
    mine_ref = fresh.at[i]
    own = held.at[z, x, i, c]
    along_z = [copies.start(mine_ref, own, z_peer(k)) for k in range(1, zs)]
    to_x, to_inner, to_core = [], [], []
    for k in range(zs):
        from_z = lax.rem(z + zs - k, zs)
        slot = held.at[from_z, x, i, c]
        if k > 0:
            along_z[k - 1].wait_recv()
        src = mine_ref if k == 0 else slot
        to_x.append(copies.start(src, slot, x_peer))
        to_inner.append([copies.start(src, slot, inner_peer(m)) for m in range(1, inner)])
        to_core.append(copies.start(src, slot, core_peer))
        if work:
            work.pop(0)()
    held[z, x, i, c] = fresh[i]
    corner = []
    for k in range(zs):
        from_z = lax.rem(z + zs - k, zs)
        slot = held.at[from_z, 1 - x, i, c]
        to_x[k].wait_recv()
        ahead = [
            copies.start(slot.at[0], slot.at[0], inner_peer(m)) for m in range(1, inner)
        ]
        to_core.append(copies.start(slot, slot, core_peer))
        for m in range(1, inner):
            from_i = lax.rem(i + inner - m, inner)
            slot = held.at[from_z, x, from_i, c]
            to_inner[k][m - 1].wait_recv()
            across = copies.start(slot.at[1], slot.at[1], x_peer)
            to_core.append(copies.start(slot, slot, core_peer))
            corner.append((from_z, from_i, ahead[m - 1], across))
        if work:
            work.pop(0)()
    for task in work:
        task()
    for from_z, from_i, ahead, across in corner:
        slot = held.at[from_z, 1 - x, from_i, c]
        ahead.wait_recv()
        to_core.append(copies.start(slot.at[0], slot.at[0], core_peer))
        across.wait_recv()
        to_core.append(copies.start(slot.at[1], slot.at[1], core_peer))
    for copy in to_core:
        copy.wait_recv()

    @pl.loop(0, nb)
    def _(b):
        d, bk = owner_ref[b], jnp.minimum(number_ref[b], cap - 1)
        bz, bx, bc = d // (XS * CORES), lax.rem(d // CORES, XS), lax.rem(d, CORES)
        for part in range(inner):
            for h in range(2):
                lo = (part * 2 + h) * wide
                out_ref[b, lo : lo + wide, :] = held[bz, bx, part, bc, h, bk]

    copies.finish()


def local(grad_parts, owner, *state):
    zs = lax.axis_size("dp") // (XS * CORES)
    inner = lax.axis_size("inner")
    nb, order = grad_parts.shape[1], grad_parts.shape[2]
    cap = state[0].shape[0]
    rows = order // (CORES * XS * inner)
    wide = order // (inner * 2)
    half = nb // 2
    plane = XS * CORES * cap
    f32, bf16 = jnp.float32, jnp.bfloat16
    tile = (rows, order)
    g = grad_parts.reshape(nb, CORES, XS, inner, rows, order)
    offsets = len(plane_offsets(inner))
    others = inner - 1
    count = PIECES + PIECES * inner + (zs - 1) + offsets
    count += (zs - 1) + zs * (2 + others) + zs * (1 + 3 * others) + zs * 2 * others
    smem = pl.BlockSpec(memory_space=pltpu.SMEM)
    vmem = pl.BlockSpec(memory_space=pltpu.VMEM)
    anywhere = pl.BlockSpec(memory_space=pl.ANY)
    square = jax.ShapeDtypeStruct((cap, order, order), f32)
    return pl.pallas_call(
        functools.partial(step_kernel, zs, inner, cap, nb, rows, wide),
        out_shape=(jax.ShapeDtypeStruct((nb, order, order), bf16),) + (square,) * 6,
        in_specs=[smem, vmem] + [anywhere] * 7,
        out_specs=(vmem,) * 7,
        scratch_shapes=[
            pltpu.SMEM((zs * plane,), jnp.int32),
            pltpu.SMEM((nb,), jnp.int32),
        ]
        + [pltpu.VMEM((cap, order, order), a.dtype) for a in state]
        + [
            pltpu.VMEM((nb, XS, inner) + tile, bf16),
            pltpu.VMEM((nb, XS, inner) + tile, bf16),
            pltpu.VMEM((inner - 1, half, XS) + tile, bf16),
            pltpu.VMEM((half, XS) + tile, bf16),
            pltpu.VMEM((half, XS) + tile, f32),
            pltpu.VMEM((half,) + tile, bf16),
            pltpu.VMEM((half, inner) + tile, bf16),
            pltpu.VMEM((half, inner) + tile, bf16),
            pltpu.VMEM((half, inner) + tile, f32),
            pltpu.VMEM((inner - 1, half) + tile, bf16),
            pltpu.VMEM((nb,) + tile, f32),
            pltpu.VMEM((zs - 1, plane) + tile, bf16),
            pltpu.VMEM((plane,) + tile, f32),
            pltpu.VMEM((zs - 1, plane) + tile, bf16),
            pltpu.VMEM((plane,) + tile, bf16),
            pltpu.VMEM((CORES * XS * inner, cap) + tile, bf16),
            pltpu.VMEM((cap, order, order), f32),
            pltpu.VMEM((inner, 2, cap, wide, order), bf16),
            pltpu.VMEM((zs, XS, inner, CORES, 2, cap, wide, order), bf16),
            pltpu.SemaphoreType.DMA((7,)),
            pltpu.SemaphoreType.DMA((count,)),
            pltpu.SemaphoreType.DMA((count,)),
        ],
        compiler_params=pltpu.CompilerParams(
            collective_id=0, has_side_effects=True, vmem_limit_bytes=60 * 1024 * 1024
        ),
    )(owner, g, *state)


def solution(mesh):
    dp = P("dp", None, None)
    in_specs = (P(("dp", "inner"), None, None, None), P()) + (dp,) * 7
    out_specs = (P(),) + (dp,) * 6
    return jax.shard_map(local, mesh=mesh, in_specs=in_specs, out_specs=out_specs, check_vma=False)
```

```python
import functools

import jax
import jax.numpy as jnp
from jax import lax
from jax.experimental import pallas as pl
from jax.experimental.pallas import tpu as pltpu
from jax.sharding import PartitionSpec as P

NS_STEPS = 5


SMOOTHING = 0.95
BIAS_CORRECTION = 1.0 - 0.95**10
LEARNING_RATE = 0.01
MESH = pl.DeviceIdType.MESH
CORES = 2
XS = 2
PIECES = 10


def position(inner_count):
    d = lax.axis_index("dp")
    c = lax.rem(d, CORES)
    x = lax.rem(d // CORES, XS)
    z = d // (CORES * XS)
    i = lax.axis_index("inner")
    return z, x, c, i


def dp_of(z, x, c):
    return (z * XS + x) * CORES + c


class Copies:
    def __init__(self, send, recv):
        self.send, self.recv, self.made = send, recv, []

    def start(self, src, dst, device):
        n = len(self.made)
        copy = pltpu.make_async_remote_copy(
            src_ref=src,
            dst_ref=dst,
            send_sem=self.send.at[n],
            recv_sem=self.recv.at[n],
            device_id=device,
            device_id_type=MESH,
        )
        copy.start()
        self.made.append(copy)
        return copy

    def finish(self):
        for copy in self.made:
            copy.wait_send()


def greet(devices):
    barrier = pltpu.get_barrier_semaphore()
    for device in devices:
        pl.semaphore_signal(barrier, inc=1, device_id=device, device_id_type=MESH)
    pl.semaphore_wait(barrier, len(devices))


def plane_offsets(inner_count):
    return [
        (dx, dc, di)
        for di in range(inner_count)
        for dx in range(XS)
        for dc in range(CORES)
        if (dx, dc, di) != (0, 0, 0)
    ]


def parts_of(value):
    high = value.astype(jnp.bfloat16)
    return high, (value - high.astype(jnp.float32)).astype(jnp.bfloat16)


def product(left, right, dims):
    def dot(a, b):
        return lax.dot_general(a, b, (dims, ((), ())), preferred_element_type=jnp.float32)

    total = dot(left[0], right[0])
    if len(right) > 1:
        total = total + dot(left[0], right[1])
    if len(left) > 1:
        total = total + dot(left[1], right[0])
    return total


PLAIN = ((1,), (0,))
LEFT_T = ((0,), (0,))
RIGHT_T = ((1,), (1,))


def step_kernel(
    zs, inner, cap, nb, rows, wide,
    owner_ref, g_hbm, w_hbm, m1_hbm, m2_hbm, ls_hbm, rs_hbm, lb_hbm, rb_hbm,
    out_ref, m1_ref, m2_ref, ls_ref, rs_ref, lb_ref, rb_ref,
    block_ref, number_ref, g_ref,
    w_in, m1_in, m2_in, ls_in, rs_in, lb_in, rb_in,
    b1, s1, r2a, s2a, f2a, r3a, r2b, s2b, f2b, r3b, total, zsend, zown, zrecv, psend, gbuf,
    grads, fresh, held,
    load, send, recv,
):
    z, x, c, i = position(inner)
    f32, bf16 = jnp.float32, jnp.bfloat16
    here = dp_of(z, x, c)
    core_peer = (dp_of(z, x, 1 - c), i)
    x_peer = (dp_of(z, 1 - x, c), i)

    def inner_peer(m):
        return (here, lax.rem(i + m, inner))

    def z_peer(k):
        return (dp_of(lax.rem(z + k, zs), x, c), i)

    def plane_peer(dx, dc, di):
        return (dp_of(z, lax.rem(x + dx, XS), lax.rem(c + dc, CORES)), lax.rem(i + di, inner))

    offsets = plane_offsets(inner)
    loads = []
    for n, (src, dst) in enumerate([
        (w_hbm, w_in), (m1_hbm, m1_in), (m2_hbm, m2_in), (ls_hbm, ls_in),
        (rs_hbm, rs_in), (lb_hbm, lb_in), (rb_hbm, rb_in),
    ]):
        loads.append(pltpu.make_async_copy(src, dst, load.at[n]))
    own_grads = pltpu.make_async_copy(g_hbm.at[:, c], g_ref, load.at[7])
    own_grads.start()
    greet([plane_peer(*o) for o in offsets] + [z_peer(k) for k in range(1, zs)])

    copies = Copies(send, recv)
    half = nb // 2
    size = nb // PIECES
    pieces = []
    for p in range(PIECES // 2):
        pieces += [(True, p * size), (False, half + p * size)]

    first = [
        copies.start(g_hbm.at[pl.ds(lo, size), 1 - c], b1.at[pl.ds(lo, size)], core_peer)
        for _, lo in pieces
    ]
    for copy in loads:
        copy.start()

    @pl.loop(0, zs * XS * CORES)
    def _(d):
        def look(b, state):
            seen, found = state
            hit = owner_ref[b] == d
            found = tuple(
                jnp.where(hit & (seen == n), b, old) for n, old in enumerate(found)
            )
            return seen + jnp.where(hit, 1, 0), found

        none = tuple(jnp.int32(-1) for _ in range(cap))
        _, found = lax.fori_loop(0, nb, look, (jnp.int32(0), none))
        for n in range(cap):
            block_ref[d * cap + n] = found[n]

    @pl.loop(0, nb)
    def _(b):
        def look(other, seen):
            return seen + jnp.where((owner_ref[other] == owner_ref[b]) & (other < b), 1, 0)

        number_ref[b] = lax.fori_loop(0, nb, look, jnp.int32(0))

    own_grads.wait()
    second = []
    for (inner_first, lo), arrived in zip(pieces, first):
        arrived.wait_recv()

        @pl.loop(lo, lo + size)
        def _(b):
            s1[b] = (g_ref[b].astype(f32) + b1[b].astype(f32)).astype(bf16)

        if inner_first:
            second.append([
                copies.start(
                    s1.at[pl.ds(lo, size), :, lax.rem(i + m, inner)],
                    r2a.at[m - 1, pl.ds(lo, size)],
                    inner_peer(m),
                )
                for m in range(1, inner)
            ])
        else:
            second.append([
                copies.start(
                    s1.at[pl.ds(lo, size), 1 - x], r2b.at[pl.ds(lo - half, size)], x_peer
                )
            ])
    third = []
    for (inner_first, lo), arrived in zip(pieces, second):
        for copy in arrived:
            copy.wait_recv()
        if inner_first:

            @pl.loop(lo, lo + size)
            def _(b):
                value = g_ref[b, :, i].astype(f32) + b1[b, :, i].astype(f32)
                for m in range(1, inner):
                    value = value + r2a[m - 1, b].astype(f32)
                f2a[b] = value
                s2a[b] = value.astype(bf16)

            third.append([
                copies.start(s2a.at[pl.ds(lo, size), 1 - x], r3a.at[pl.ds(lo, size)], x_peer)
            ])
        else:

            @pl.loop(lo, lo + size)
            def _(b):
                value = g_ref[b, x].astype(f32) + b1[b, x].astype(f32)
                value = value + r2b[b - half].astype(f32)
                f2b[b - half] = value
                s2b[b - half] = value.astype(bf16)

            third.append([
                copies.start(
                    s2b.at[pl.ds(lo - half, size), lax.rem(i + m, inner)],
                    r3b.at[m - 1, pl.ds(lo - half, size)],
                    inner_peer(m),
                )
                for m in range(1, inner)
            ])
    for (inner_first, lo), arrived in zip(pieces, third):
        for copy in arrived:
            copy.wait_recv()
        if inner_first:

            @pl.loop(lo, lo + size)
            def _(b):
                total[b] = f2a[b, x] + r3a[b].astype(f32)

        else:

            @pl.loop(lo, lo + size)
            def _(b):
                value = f2b[b - half, i]
                for m in range(1, inner):
                    value = value + r3b[m - 1, b - half].astype(f32)
                total[b] = value

    plane = XS * CORES * cap

    def slot_value(slot):
        block = block_ref[slot]
        value = total[jnp.maximum(block, 0)]
        return jnp.where(block >= 0, value, jnp.zeros_like(value))

    fourth = []
    for k in range(1, zs):
        there = lax.rem(z + k, zs)

        @pl.loop(0, plane)
        def _(s):
            zsend[k - 1, s] = slot_value(there * plane + s).astype(bf16)

        fourth.append(copies.start(zsend.at[k - 1], zrecv.at[k - 1], z_peer(k)))

    @pl.loop(0, plane)
    def _(s):
        zown[s] = slot_value(z * plane + s)

    for copy in fourth:
        copy.wait_recv()

    @pl.loop(0, plane)
    def _(s):
        value = zown[s]
        for k in range(1, zs):
            value = value + zrecv[k - 1, s].astype(f32)
        psend[s] = value.astype(bf16)

    share = (c * XS + x) * inner + i
    fifth = []
    for dx, dc, di in offsets:
        to = lax.rem(x + dx, XS) * CORES + lax.rem(c + dc, CORES)
        fifth.append(
            copies.start(
                psend.at[pl.ds(to * cap, cap)], gbuf.at[share], plane_peer(dx, dc, di)
            )
        )
    gbuf[share] = psend[pl.ds((x * CORES + c) * cap, cap)]
    for copy in fifth:
        copy.wait_recv()
    for s in range(CORES * XS * inner):
        grads[:, s * rows : (s + 1) * rows, :] = gbuf[s].astype(f32)
    for copy in loads:
        copy.wait()

    for k in range(cap):
        lb, rb = parts_of(lb_in[k]), parts_of(rb_in[k])
        half_turn = product(lb, (grads[k].astype(bf16),), LEFT_T)
        rotated = product(parts_of(half_turn), rb, PLAIN)
        first = SMOOTHING * m1_in[k] + (1.0 - SMOOTHING) * rotated
        second = SMOOTHING * m2_in[k] + (1.0 - SMOOTHING) * rotated * rotated
        m1_ref[k] = first
        m2_ref[k] = second
        direction = first / BIAS_CORRECTION / (jnp.sqrt(second / BIAS_CORRECTION) + 1e-08)
        back_turn = product(lb, parts_of(direction), PLAIN)
        update = product(parts_of(back_turn), rb, RIGHT_T)
        new = (w_in[k].astype(f32) - LEARNING_RATE * update).astype(bf16)
        for part in range(inner):
            for h in range(2):
                lo = (part * 2 + h) * wide
                fresh[part, h, k] = new[lo : lo + wide]

    def powers():
        @pl.loop(0, cap)
        def _(k):
            g = (grads[k].astype(bf16),)
            for in_ref, stats_ref, basis_in, basis_ref, dims in (
                (ls_in, ls_ref, lb_in, lb_ref, RIGHT_T),
                (rs_in, rs_ref, rb_in, rb_ref, LEFT_T),
            ):
                stats = SMOOTHING * in_ref[k] + (1.0 - SMOOTHING) * product(g, g, dims)
                stats_ref[k] = stats
                power = product(parts_of(stats), parts_of(basis_in[k]), PLAIN)
                norm = jnp.sqrt(jnp.sum(power * power, axis=(0, 1), keepdims=True))
                basis_ref[k] = power / (norm + 1e-06)

    def newton_schulz():
        @pl.loop(0, cap)
        def _(k):
            for basis_ref in (lb_ref, rb_ref):
                current = basis_ref[k]
                parts = parts_of(current)
                square = product(parts, parts, RIGHT_T)
                cubic = product(parts_of(square), parts, PLAIN)
                basis_ref[k] = 1.5 * current - 0.5 * cubic

    work = [powers] + [newton_schulz] * NS_STEPS
    mine_ref = fresh.at[i]
    own = held.at[z, x, i, c]
    along_z = [copies.start(mine_ref, own, z_peer(k)) for k in range(1, zs)]
    to_x, to_inner, to_core = [], [], []
    for k in range(zs):
        from_z = lax.rem(z + zs - k, zs)
        slot = held.at[from_z, x, i, c]
        if k > 0:
            along_z[k - 1].wait_recv()
        src = mine_ref if k == 0 else slot
        to_x.append(copies.start(src, slot, x_peer))
        to_inner.append([copies.start(src, slot, inner_peer(m)) for m in range(1, inner)])
        to_core.append(copies.start(src, slot, core_peer))
        if work:
            work.pop(0)()
    held[z, x, i, c] = fresh[i]
    corner = []
    for k in range(zs):
        from_z = lax.rem(z + zs - k, zs)
        slot = held.at[from_z, 1 - x, i, c]
        to_x[k].wait_recv()
        ahead = [
            copies.start(slot.at[0], slot.at[0], inner_peer(m)) for m in range(1, inner)
        ]
        to_core.append(copies.start(slot, slot, core_peer))
        for m in range(1, inner):
            from_i = lax.rem(i + inner - m, inner)
            slot = held.at[from_z, x, from_i, c]
            to_inner[k][m - 1].wait_recv()
            across = copies.start(slot.at[1], slot.at[1], x_peer)
            to_core.append(copies.start(slot, slot, core_peer))
            corner.append((from_z, from_i, ahead[m - 1], across))
        if work:
            work.pop(0)()
    for task in work:
        task()
    for from_z, from_i, ahead, across in corner:
        slot = held.at[from_z, 1 - x, from_i, c]
        ahead.wait_recv()
        to_core.append(copies.start(slot.at[0], slot.at[0], core_peer))
        across.wait_recv()
        to_core.append(copies.start(slot.at[1], slot.at[1], core_peer))
    for copy in to_core:
        copy.wait_recv()

    @pl.loop(0, nb)
    def _(b):
        d, bk = owner_ref[b], jnp.minimum(number_ref[b], cap - 1)
        bz, bx, bc = d // (XS * CORES), lax.rem(d // CORES, XS), lax.rem(d, CORES)
        for part in range(inner):
            for h in range(2):
                lo = (part * 2 + h) * wide
                out_ref[b, lo : lo + wide, :] = held[bz, bx, part, bc, h, bk]

    copies.finish()


def finish_kernel(*refs):
    done = refs[14]
    copies = [pltpu.make_async_copy(refs[n], refs[7 + n], done.at[n]) for n in range(7)]
    for copy in copies:
        copy.start()
    for copy in copies:
        copy.wait()


def local(grad_parts, owner, *state):
    zs = lax.axis_size("dp") // (XS * CORES)
    inner = lax.axis_size("inner")
    nb, order = grad_parts.shape[1], grad_parts.shape[2]
    cap = state[0].shape[0]
    rows = order // (CORES * XS * inner)
    wide = order // (inner * 2)
    half = nb // 2
    plane = XS * CORES * cap
    f32, bf16 = jnp.float32, jnp.bfloat16
    tile = (rows, order)
    g = grad_parts.reshape(nb, CORES, XS, inner, rows, order)
    offsets = len(plane_offsets(inner))
    others = inner - 1
    count = PIECES + PIECES * inner + (zs - 1) + offsets
    count += (zs - 1) + zs * (2 + others) + zs * (1 + 3 * others) + zs * 2 * others
    smem = pl.BlockSpec(memory_space=pltpu.SMEM)
    vmem = pl.BlockSpec(memory_space=pltpu.VMEM)
    anywhere = pl.BlockSpec(memory_space=pl.ANY)
    square = jax.ShapeDtypeStruct((cap, order, order), f32)
    shapes = (jax.ShapeDtypeStruct((nb, order, order), bf16),) + (square,) * 6
    results = pl.pallas_call(
        functools.partial(step_kernel, zs, inner, cap, nb, rows, wide),
        out_shape=(pltpu.VMEM((nb, order, order), bf16),) + (pltpu.VMEM((cap, order, order), f32),) * 6,
        in_specs=[smem] + [anywhere] * 8,
        out_specs=(vmem,) * 7,
        scratch_shapes=[
            pltpu.SMEM((zs * plane,), jnp.int32),
            pltpu.SMEM((nb,), jnp.int32),
            pltpu.VMEM((nb, XS, inner) + tile, bf16),
        ]
        + [pltpu.VMEM((cap, order, order), a.dtype) for a in state]
        + [
            pltpu.VMEM((nb, XS, inner) + tile, bf16),
            pltpu.VMEM((nb, XS, inner) + tile, bf16),
            pltpu.VMEM((inner - 1, half, XS) + tile, bf16),
            pltpu.VMEM((half, XS) + tile, bf16),
            pltpu.VMEM((half, XS) + tile, f32),
            pltpu.VMEM((half,) + tile, bf16),
            pltpu.VMEM((half, inner) + tile, bf16),
            pltpu.VMEM((half, inner) + tile, bf16),
            pltpu.VMEM((half, inner) + tile, f32),
            pltpu.VMEM((inner - 1, half) + tile, bf16),
            pltpu.VMEM((nb,) + tile, f32),
            pltpu.VMEM((zs - 1, plane) + tile, bf16),
            pltpu.VMEM((plane,) + tile, f32),
            pltpu.VMEM((zs - 1, plane) + tile, bf16),
            pltpu.VMEM((plane,) + tile, bf16),
            pltpu.VMEM((CORES * XS * inner, cap) + tile, bf16),
            pltpu.VMEM((cap, order, order), f32),
            pltpu.VMEM((inner, 2, cap, wide, order), bf16),
            pltpu.VMEM((zs, XS, inner, CORES, 2, cap, wide, order), bf16),
            pltpu.SemaphoreType.DMA((8,)),
            pltpu.SemaphoreType.DMA((count,)),
            pltpu.SemaphoreType.DMA((count,)),
        ],
        compiler_params=pltpu.CompilerParams(
            collective_id=0, has_side_effects=True, vmem_limit_bytes=58 * 1024 * 1024
        ),
    )(owner, g, *state)
    return pl.pallas_call(
        finish_kernel,
        out_shape=shapes,
        in_specs=[anywhere] * 7,
        out_specs=(anywhere,) * 7,
        scratch_shapes=[pltpu.SemaphoreType.DMA((7,))],
        compiler_params=pltpu.CompilerParams(vmem_limit_bytes=1024 * 1024),
    )(*results)


def solution(mesh):
    dp = P("dp", None, None)
    in_specs = (P(("dp", "inner"), None, None, None), P()) + (dp,) * 7
    out_specs = (P(),) + (dp,) * 6
    return jax.shard_map(local, mesh=mesh, in_specs=in_specs, out_specs=out_specs, check_vma=False)
```

```python
import functools

import jax
import jax.numpy as jnp
from jax import lax
from jax.experimental import pallas as pl
from jax.experimental.pallas import tpu as pltpu
from jax.sharding import PartitionSpec as P

NS_STEPS = 5


SMOOTHING = 0.95
BIAS_CORRECTION = 1.0 - 0.95**10
LEARNING_RATE = 0.01
MESH = pl.DeviceIdType.MESH
CORES = 2
XS = 2
PIECES = 10


def position(inner_count):
    d = lax.axis_index("dp")
    c = lax.rem(d, CORES)
    x = lax.rem(d // CORES, XS)
    z = d // (CORES * XS)
    i = lax.axis_index("inner")
    return z, x, c, i


def dp_of(z, x, c):
    return (z * XS + x) * CORES + c


class Copies:
    def __init__(self, send, recv):
        self.send, self.recv, self.made = send, recv, []

    def start(self, src, dst, device):
        n = len(self.made)
        copy = pltpu.make_async_remote_copy(
            src_ref=src,
            dst_ref=dst,
            send_sem=self.send.at[n],
            recv_sem=self.recv.at[n],
            device_id=device,
            device_id_type=MESH,
        )
        copy.start()
        self.made.append(copy)
        return copy

    def finish(self):
        for copy in self.made:
            copy.wait_send()


def greet(devices):
    barrier = pltpu.get_barrier_semaphore()
    for device in devices:
        pl.semaphore_signal(barrier, inc=1, device_id=device, device_id_type=MESH)
    pl.semaphore_wait(barrier, len(devices))


def plane_offsets(inner_count):
    return [
        (dx, dc, di)
        for di in range(inner_count)
        for dx in range(XS)
        for dc in range(CORES)
        if (dx, dc, di) != (0, 0, 0)
    ]


def parts_of(value):
    high = value.astype(jnp.bfloat16)
    return high, (value - high.astype(jnp.float32)).astype(jnp.bfloat16)


def product(left, right, dims):
    def dot(a, b):
        return lax.dot_general(a, b, (dims, ((), ())), preferred_element_type=jnp.float32)

    total = dot(left[0], right[0])
    if len(right) > 1:
        total = total + dot(left[0], right[1])
    if len(left) > 1:
        total = total + dot(left[1], right[0])
    return total


PLAIN = ((1,), (0,))
LEFT_T = ((0,), (0,))
RIGHT_T = ((1,), (1,))


def step_kernel(
    zs, inner, cap, nb, rows, wide,
    owner_ref, g_hbm, w_hbm, m1_hbm, m2_hbm, ls_hbm, rs_hbm, lb_hbm, rb_hbm,
    out_ref, m1_ref, m2_ref, ls_ref, rs_ref, lb_ref, rb_ref,
    block_ref, number_ref, g_ref,
    w_in, m1_in, m2_in, ls_in, rs_in, lb_in, rb_in,
    b1, s1, r2a, s2a, f2a, r3a, r2b, s2b, f2b, r3b, total, zsend, zown, zrecv, psend, gbuf,
    grads, fresh, held,
    load, send, recv,
):
    z, x, c, i = position(inner)
    f32, bf16 = jnp.float32, jnp.bfloat16
    here = dp_of(z, x, c)
    core_peer = (dp_of(z, x, 1 - c), i)
    x_peer = (dp_of(z, 1 - x, c), i)

    def inner_peer(m):
        return (here, lax.rem(i + m, inner))

    def z_peer(k):
        return (dp_of(lax.rem(z + k, zs), x, c), i)

    def plane_peer(dx, dc, di):
        return (dp_of(z, lax.rem(x + dx, XS), lax.rem(c + dc, CORES)), lax.rem(i + di, inner))

    offsets = plane_offsets(inner)
    loads = []
    for n, (src, dst) in enumerate([
        (w_hbm, w_in), (m1_hbm, m1_in), (m2_hbm, m2_in), (ls_hbm, ls_in),
        (rs_hbm, rs_in), (lb_hbm, lb_in), (rb_hbm, rb_in),
    ]):
        loads.append(pltpu.make_async_copy(src, dst, load.at[n]))
    own_grads = pltpu.make_async_copy(g_hbm.at[:, c], g_ref, load.at[7])
    own_grads.start()
    greet([plane_peer(*o) for o in offsets] + [z_peer(k) for k in range(1, zs)])

    copies = Copies(send, recv)
    half = nb // 2
    size = nb // PIECES
    pieces = []
    for p in range(PIECES // 2):
        pieces += [(True, p * size), (False, half + p * size)]

    first = [
        copies.start(g_hbm.at[pl.ds(lo, size), 1 - c], b1.at[pl.ds(lo, size)], core_peer)
        for _, lo in pieces
    ]
    for copy in loads:
        copy.start()

    @pl.loop(0, zs * XS * CORES)
    def _(d):
        def look(b, state):
            seen, found = state
            hit = owner_ref[b] == d
            found = tuple(
                jnp.where(hit & (seen == n), b, old) for n, old in enumerate(found)
            )
            return seen + jnp.where(hit, 1, 0), found

        none = tuple(jnp.int32(-1) for _ in range(cap))
        _, found = lax.fori_loop(0, nb, look, (jnp.int32(0), none))
        for n in range(cap):
            block_ref[d * cap + n] = found[n]

    @pl.loop(0, nb)
    def _(b):
        def look(other, seen):
            return seen + jnp.where((owner_ref[other] == owner_ref[b]) & (other < b), 1, 0)

        number_ref[b] = lax.fori_loop(0, nb, look, jnp.int32(0))

    own_grads.wait()
    second = []
    for (inner_first, lo), arrived in zip(pieces, first):
        arrived.wait_recv()

        @pl.loop(lo, lo + size)
        def _(b):
            s1[b] = (g_ref[b].astype(f32) + b1[b].astype(f32)).astype(bf16)

        if inner_first:
            second.append([
                copies.start(
                    s1.at[pl.ds(lo, size), :, lax.rem(i + m, inner)],
                    r2a.at[m - 1, pl.ds(lo, size)],
                    inner_peer(m),
                )
                for m in range(1, inner)
            ])
        else:
            second.append([
                copies.start(
                    s1.at[pl.ds(lo, size), 1 - x], r2b.at[pl.ds(lo - half, size)], x_peer
                )
            ])
    third = []
    for (inner_first, lo), arrived in zip(pieces, second):
        for copy in arrived:
            copy.wait_recv()
        if inner_first:

            @pl.loop(lo, lo + size)
            def _(b):
                value = g_ref[b, :, i].astype(f32) + b1[b, :, i].astype(f32)
                for m in range(1, inner):
                    value = value + r2a[m - 1, b].astype(f32)
                f2a[b] = value
                s2a[b] = value.astype(bf16)

            third.append([
                copies.start(s2a.at[pl.ds(lo, size), 1 - x], r3a.at[pl.ds(lo, size)], x_peer)
            ])
        else:

            @pl.loop(lo, lo + size)
            def _(b):
                value = g_ref[b, x].astype(f32) + b1[b, x].astype(f32)
                value = value + r2b[b - half].astype(f32)
                f2b[b - half] = value
                s2b[b - half] = value.astype(bf16)

            third.append([
                copies.start(
                    s2b.at[pl.ds(lo - half, size), lax.rem(i + m, inner)],
                    r3b.at[m - 1, pl.ds(lo - half, size)],
                    inner_peer(m),
                )
                for m in range(1, inner)
            ])
    for (inner_first, lo), arrived in zip(pieces, third):
        for copy in arrived:
            copy.wait_recv()
        if inner_first:

            @pl.loop(lo, lo + size)
            def _(b):
                total[b] = f2a[b, x] + r3a[b].astype(f32)

        else:

            @pl.loop(lo, lo + size)
            def _(b):
                value = f2b[b - half, i]
                for m in range(1, inner):
                    value = value + r3b[m - 1, b - half].astype(f32)
                total[b] = value

    plane = XS * CORES * cap

    def slot_value(slot):
        block = block_ref[slot]
        value = total[jnp.maximum(block, 0)]
        return jnp.where(block >= 0, value, jnp.zeros_like(value))

    fourth = []
    for k in range(1, zs):
        there = lax.rem(z + k, zs)

        @pl.loop(0, plane)
        def _(s):
            zsend[k - 1, s] = slot_value(there * plane + s).astype(bf16)

        fourth.append(copies.start(zsend.at[k - 1], zrecv.at[k - 1], z_peer(k)))

    @pl.loop(0, plane)
    def _(s):
        zown[s] = slot_value(z * plane + s)

    for copy in fourth:
        copy.wait_recv()

    @pl.loop(0, plane)
    def _(s):
        value = zown[s]
        for k in range(1, zs):
            value = value + zrecv[k - 1, s].astype(f32)
        psend[s] = value.astype(bf16)

    share = (c * XS + x) * inner + i
    fifth = []
    for dx, dc, di in offsets:
        to = lax.rem(x + dx, XS) * CORES + lax.rem(c + dc, CORES)
        fifth.append(
            copies.start(
                psend.at[pl.ds(to * cap, cap)], gbuf.at[share], plane_peer(dx, dc, di)
            )
        )
    gbuf[share] = psend[pl.ds((x * CORES + c) * cap, cap)]
    for copy in fifth:
        copy.wait_recv()
    for s in range(CORES * XS * inner):
        grads[:, s * rows : (s + 1) * rows, :] = gbuf[s].astype(f32)
    for copy in loads:
        copy.wait()

    for k in range(cap):
        lb, rb = parts_of(lb_in[k]), parts_of(rb_in[k])
        half_turn = product(lb, (grads[k].astype(bf16),), LEFT_T)
        rotated = product(parts_of(half_turn), rb, PLAIN)
        first = SMOOTHING * m1_in[k] + (1.0 - SMOOTHING) * rotated
        second = SMOOTHING * m2_in[k] + (1.0 - SMOOTHING) * rotated * rotated
        m1_ref[k] = first
        m2_ref[k] = second
        direction = first / BIAS_CORRECTION / (jnp.sqrt(second / BIAS_CORRECTION) + 1e-08)
        back_turn = product(lb, parts_of(direction), PLAIN)
        update = product(parts_of(back_turn), rb, RIGHT_T)
        new = (w_in[k].astype(f32) - LEARNING_RATE * update).astype(bf16)
        for part in range(inner):
            for h in range(2):
                lo = (part * 2 + h) * wide
                fresh[part, h, k] = new[lo : lo + wide]

    def powers():
        @pl.loop(0, cap)
        def _(k):
            g = (grads[k].astype(bf16),)
            for in_ref, stats_ref, basis_in, basis_ref, dims in (
                (ls_in, ls_ref, lb_in, lb_ref, RIGHT_T),
                (rs_in, rs_ref, rb_in, rb_ref, LEFT_T),
            ):
                stats = SMOOTHING * in_ref[k] + (1.0 - SMOOTHING) * product(g, g, dims)
                stats_ref[k] = stats
                power = product(parts_of(stats), parts_of(basis_in[k]), PLAIN)
                norm = jnp.sqrt(jnp.sum(power * power, axis=(0, 1), keepdims=True))
                basis_ref[k] = power / (norm + 1e-06)

    def newton_schulz():
        @pl.loop(0, cap)
        def _(k):
            for basis_ref in (lb_ref, rb_ref):
                current = basis_ref[k]
                parts = parts_of(current)
                square = product(parts, parts, RIGHT_T)
                cubic = product(parts_of(square), parts, PLAIN)
                basis_ref[k] = 1.5 * current - 0.5 * cubic

    work = [powers] + [newton_schulz] * NS_STEPS
    mine_ref = fresh.at[i]
    own = held.at[z, x, i, c]
    along_z = [copies.start(mine_ref, own, z_peer(k)) for k in range(1, zs)]
    to_x, to_inner, to_core, corner = [], [], [], []

    def forward(k):
        from_z = lax.rem(z + zs - k, zs)
        slot = held.at[from_z, 1 - x, i, c]
        to_x[k].wait_recv()
        ahead = [
            copies.start(slot.at[0], slot.at[0], inner_peer(m)) for m in range(1, inner)
        ]
        to_core.append(copies.start(slot, slot, core_peer))
        for m in range(1, inner):
            from_i = lax.rem(i + inner - m, inner)
            slot = held.at[from_z, x, from_i, c]
            to_inner[k][m - 1].wait_recv()
            across = copies.start(slot.at[1], slot.at[1], x_peer)
            to_core.append(copies.start(slot, slot, core_peer))
            corner.append((from_z, from_i, ahead[m - 1], across))

    for k in range(zs):
        from_z = lax.rem(z + zs - k, zs)
        slot = held.at[from_z, x, i, c]
        if k > 0:
            along_z[k - 1].wait_recv()
        src = mine_ref if k == 0 else slot
        to_x.append(copies.start(src, slot, x_peer))
        to_inner.append([copies.start(src, slot, inner_peer(m)) for m in range(1, inner)])
        to_core.append(copies.start(src, slot, core_peer))
        if work:
            work.pop(0)()
        if k > 0:
            forward(k - 1)
            if work:
                work.pop(0)()
    held[z, x, i, c] = fresh[i]
    forward(zs - 1)
    for task in work:
        task()
    for from_z, from_i, ahead, across in corner:
        slot = held.at[from_z, 1 - x, from_i, c]
        ahead.wait_recv()
        to_core.append(copies.start(slot.at[0], slot.at[0], core_peer))
        across.wait_recv()
        to_core.append(copies.start(slot.at[1], slot.at[1], core_peer))
    for copy in to_core:
        copy.wait_recv()

    @pl.loop(0, nb)
    def _(b):
        d, bk = owner_ref[b], jnp.minimum(number_ref[b], cap - 1)
        bz, bx, bc = d // (XS * CORES), lax.rem(d // CORES, XS), lax.rem(d, CORES)
        for part in range(inner):
            for h in range(2):
                lo = (part * 2 + h) * wide
                out_ref[b, lo : lo + wide, :] = held[bz, bx, part, bc, h, bk]

    copies.finish()


def finish_kernel(*refs):
    done = refs[14]
    copies = [pltpu.make_async_copy(refs[n], refs[7 + n], done.at[n]) for n in range(7)]
    for copy in copies:
        copy.start()
    for copy in copies:
        copy.wait()


def local(grad_parts, owner, *state):
    zs = lax.axis_size("dp") // (XS * CORES)
    inner = lax.axis_size("inner")
    nb, order = grad_parts.shape[1], grad_parts.shape[2]
    cap = state[0].shape[0]
    rows = order // (CORES * XS * inner)
    wide = order // (inner * 2)
    half = nb // 2
    plane = XS * CORES * cap
    f32, bf16 = jnp.float32, jnp.bfloat16
    tile = (rows, order)
    g = grad_parts.reshape(nb, CORES, XS, inner, rows, order)
    offsets = len(plane_offsets(inner))
    others = inner - 1
    count = PIECES + PIECES * inner + (zs - 1) + offsets
    count += (zs - 1) + zs * (2 + others) + zs * (1 + 3 * others) + zs * 2 * others
    smem = pl.BlockSpec(memory_space=pltpu.SMEM)
    vmem = pl.BlockSpec(memory_space=pltpu.VMEM)
    anywhere = pl.BlockSpec(memory_space=pl.ANY)
    square = jax.ShapeDtypeStruct((cap, order, order), f32)
    shapes = (jax.ShapeDtypeStruct((nb, order, order), bf16),) + (square,) * 6
    results = pl.pallas_call(
        functools.partial(step_kernel, zs, inner, cap, nb, rows, wide),
        out_shape=(pltpu.VMEM((nb, order, order), bf16),) + (pltpu.VMEM((cap, order, order), f32),) * 6,
        in_specs=[smem] + [anywhere] * 8,
        out_specs=(vmem,) * 7,
        scratch_shapes=[
            pltpu.SMEM((zs * plane,), jnp.int32),
            pltpu.SMEM((nb,), jnp.int32),
            pltpu.VMEM((nb, XS, inner) + tile, bf16),
        ]
        + [pltpu.VMEM((cap, order, order), a.dtype) for a in state]
        + [
            pltpu.VMEM((nb, XS, inner) + tile, bf16),
            pltpu.VMEM((nb, XS, inner) + tile, bf16),
            pltpu.VMEM((inner - 1, half, XS) + tile, bf16),
            pltpu.VMEM((half, XS) + tile, bf16),
            pltpu.VMEM((half, XS) + tile, f32),
            pltpu.VMEM((half,) + tile, bf16),
            pltpu.VMEM((half, inner) + tile, bf16),
            pltpu.VMEM((half, inner) + tile, bf16),
            pltpu.VMEM((half, inner) + tile, f32),
            pltpu.VMEM((inner - 1, half) + tile, bf16),
            pltpu.VMEM((nb,) + tile, f32),
            pltpu.VMEM((zs - 1, plane) + tile, bf16),
            pltpu.VMEM((plane,) + tile, f32),
            pltpu.VMEM((zs - 1, plane) + tile, bf16),
            pltpu.VMEM((plane,) + tile, bf16),
            pltpu.VMEM((CORES * XS * inner, cap) + tile, bf16),
            pltpu.VMEM((cap, order, order), f32),
            pltpu.VMEM((inner, 2, cap, wide, order), bf16),
            pltpu.VMEM((zs, XS, inner, CORES, 2, cap, wide, order), bf16),
            pltpu.SemaphoreType.DMA((8,)),
            pltpu.SemaphoreType.DMA((count,)),
            pltpu.SemaphoreType.DMA((count,)),
        ],
        compiler_params=pltpu.CompilerParams(
            collective_id=0, has_side_effects=True, vmem_limit_bytes=58 * 1024 * 1024
        ),
    )(owner, g, *state)
    return pl.pallas_call(
        finish_kernel,
        out_shape=shapes,
        in_specs=[anywhere] * 7,
        out_specs=(anywhere,) * 7,
        scratch_shapes=[pltpu.SemaphoreType.DMA((7,))],
        compiler_params=pltpu.CompilerParams(vmem_limit_bytes=1024 * 1024),
    )(*results)


def solution(mesh):
    dp = P("dp", None, None)
    in_specs = (P(("dp", "inner"), None, None, None), P()) + (dp,) * 7
    out_specs = (P(),) + (dp,) * 6
    return jax.shard_map(local, mesh=mesh, in_specs=in_specs, out_specs=out_specs, check_vma=False)
```
